32 devices in a mesh: groups: 2 (over x), ep: 16 (over z, y, core).
Axes of the slice: x: 2, y: 2, z: 4, core: 2. Of those that a mesh axis runs over, the one named last changes fastest.
Arguments:
- tokens: bfloat16 [512, 3072], P(('groups', 'ep')), parts along dimension 0, may hold values from -6 to 6
- routes: int32 [512, 2], P(('groups', 'ep')), parts along dimension 0, may hold values from 0 to 3, all different within a row
- route_weights: float32 [512, 2], P(('groups', 'ep')), parts along dimension 0, may hold values from 0.1 to 1
- live_counts: int32 [32], P(('groups', 'ep')), parts along dimension 0, may hold values from 8 to 16, as said below
- w_gate: bfloat16 [3072, 32768], P(None, 'ep'), may hold values from -0.109375 to 0.109375
- w_up: bfloat16 [3072, 32768], P(None, 'ep'), may hold values from -0.109375 to 0.109375
- w_down: bfloat16 [32768, 3072], P('ep'), may hold values from -0.0625 to 0.0625
Outputs:
- mixed: bfloat16 [512, 3072], P(('groups', 'ep')), parts along dimension 0
The draws below stay inside these ranges and needn't reach their ends.
There are 2 independent parts, one for each index of `groups`. The reference program is written for one: setup_inputs(seed, part) draws one part's arguments, and reference() takes and returns one part's arrays. A program takes and returns all parts, laid end to end along the dimension named above; an argument that names none is the same for every part. Nothing has to cross between parts.
Inputs may be any that keep to these rules, and one draw needn't show every extreme that they name: `routes`: each token names two different experts. The live tokens of a device are its first live_counts rows; some device has all 16 live and some has 8.
All inputs are finite; a program needn't handle non-finite values.
Results may differ from the reference program's by a relative error of at most 0.0057.
Values may be sent and summed in bfloat16 or wider, within the bound.
A program may use at most 128 MiB of HBM per device.

```python
import jax
import jax.numpy as jnp
from jax import lax

D = 3072
FF = 8192
EXPERTS = 4
TOK_DEV = 16
TOKENS = 256
N_EP = 16


def draw_live_counts(key, part):
    key_values, key_full, key_step = jax.random.split(jax.random.fold_in(key, 7), 3)
    values = jax.random.randint(key_values, (N_EP,), TOK_DEV // 2, TOK_DEV + 1)
    full_at = jax.random.randint(key_full, (), 0, N_EP)
    fewest_at = (full_at + 1 + jax.random.randint(key_step, (), 0, N_EP - 1)) % N_EP
    device_ids = jnp.arange(N_EP)
    values = jnp.where(device_ids == full_at, TOK_DEV, values)
    values = jnp.where(device_ids == fewest_at, TOK_DEV // 2, values)
    return values.astype(jnp.int32)


def block_levels(key, extent, pieces, smallest, largest):
    loudness, own = 1.0, jax.random.fold_in(key, 6)
    for dim, blocks in pieces:
        draws = jnp.exp(jax.random.uniform(jax.random.fold_in(own, dim), (blocks,), jnp.float32, smallest / len(pieces), largest / len(pieces)))
        loudness = loudness * jnp.repeat(draws, extent[dim] // blocks).reshape([-1 if axis == dim else 1 for axis in range(len(extent))])
    return loudness


def picks_of(stream_key, rows, number_of, top, lift):
    sequence = jax.random.permutation(jax.random.fold_in(stream_key, 1), number_of)
    favour = sequence
    for power in range(3):
        favour = favour * favour // number_of
    favour = favour * lift // number_of
    chance = jax.random.randint(jax.random.fold_in(stream_key, 2), (rows, number_of), 0, 4096) + favour
    fixed_rows = jax.random.permutation(jax.random.fold_in(stream_key, 3), rows)[jnp.arange(number_of) % rows]
    chance = jnp.where(jnp.arange(rows)[:, None] == fixed_rows[None, :], 1 << 14, chance)
    priority = chance * number_of + jnp.arange(number_of)
    return lax.top_k(priority.astype(jnp.int32), top)[1].astype(jnp.int32)


def bell_draw(own_key, extent, spread, bound, shards=(), kind=jnp.bfloat16):
    entries = jax.random.normal(own_key, extent, jnp.float32) * spread
    if len(shards) > 0:
        entries = block_levels(own_key, extent, shards, -0.22, 0.18) * entries
    return jnp.clip(entries, min=-bound, max=bound).astype(kind)


def setup_inputs(seed: int = 0, part: int = 0) -> dict:
    streams_of = jax.random.split(jax.random.key(seed), 8)
    own_keys = jax.random.split(jax.random.fold_in(streams_of[7], part), 8)
    tokens = bell_draw(own_keys[0], (TOKENS, D), 1.0, 6.0, ((0, 16),))
    routes = picks_of(own_keys[1], TOKENS, EXPERTS, 2, 8192)
    route_weights = jnp.clip(0.1 + 0.9 * jax.random.uniform(own_keys[2], (TOKENS, 2), jnp.float32) ** block_levels(own_keys[2], (TOKENS, 2), ((0, 16),), -0.2, 0.2), 0.1, 1.0)
    live_counts = draw_live_counts(jax.random.fold_in(jax.random.fold_in(streams_of[7], part), 71), part)
    w_gate = bell_draw(streams_of[4], (D, EXPERTS * FF), D ** -0.5, 0.109375, ((1, 16),))
    w_up = bell_draw(streams_of[5], (D, EXPERTS * FF), D ** -0.5, 0.109375, ((1, 16),))
    w_down = bell_draw(streams_of[6], (EXPERTS * FF, D), FF ** -0.5, 0.0625, ((0, 16),))
    return dict(tokens=tokens, routes=routes, route_weights=route_weights, live_counts=live_counts, w_gate=w_gate, w_up=w_up, w_down=w_down)


def expert_output(tokens_wide, w_gate, w_up, w_down, expert):
    first = expert * FF
    gate_cols = lax.dynamic_slice_in_dim(w_gate, first, FF, 1).astype(jnp.float32)
    up_cols = lax.dynamic_slice_in_dim(w_up, first, FF, 1).astype(jnp.float32)
    down_rows = lax.dynamic_slice_in_dim(w_down, first, FF, 0).astype(jnp.float32)
    gate = jnp.dot(tokens_wide, gate_cols, precision=lax.Precision.HIGHEST)
    upward = jnp.dot(tokens_wide, up_cols, precision=lax.Precision.HIGHEST)
    hidden = (jax.nn.silu(gate) * upward).astype(jnp.bfloat16)
    hidden = lax.optimization_barrier(hidden).astype(jnp.float32)
    share = FF // (N_EP // EXPERTS)

    def partner(summed, partner_id):
        offset = partner_id * share
        hidden_cols = lax.dynamic_slice_in_dim(hidden, offset, share, 1)
        weight_rows = lax.dynamic_slice_in_dim(down_rows, offset, share, 0)
        partial_value = jnp.dot(hidden_cols, weight_rows, precision=lax.Precision.HIGHEST).astype(jnp.bfloat16)
        partial_value = lax.optimization_barrier(partial_value).astype(jnp.float32)
        return summed + partial_value, None

    summed, _ = lax.scan(partner, jnp.zeros((TOKENS, D), jnp.float32), jnp.arange(N_EP // EXPERTS, dtype=jnp.int32))
    return summed


def reference(tokens, routes, route_weights, live_counts, w_gate, w_up, w_down):
    tokens_wide = tokens.astype(jnp.float32)
    outputs = lax.map(lambda expert: expert_output(tokens_wide, w_gate, w_up, w_down, expert), jnp.arange(EXPERTS, dtype=jnp.int32))
    selector = (routes[:, :, None] == jnp.arange(EXPERTS, dtype=jnp.int32)[None, None, :]).astype(jnp.float32)
    weights = jnp.sum(route_weights[:, :, None] * selector, axis=1)
    mixed = jnp.zeros((TOKENS, D), jnp.float32)
    for expert in range(EXPERTS):
        mixed = mixed + weights[:, expert][:, None] * outputs[expert]
    row_ids = jnp.arange(TOKENS, dtype=jnp.int32)
    is_live = (row_ids % TOK_DEV) < live_counts[row_ids // TOK_DEV]
    mixed = jnp.where(is_live[:, None], mixed, jnp.float32(0.0))
    return mixed.astype(jnp.bfloat16)
```

```python
import functools

import jax
import jax.numpy as jnp
from jax import lax
from jax.experimental import pallas as pl
from jax.experimental.pallas import tpu as pltpu
from jax.sharding import PartitionSpec as P

MESH = pl.DeviceIdType.MESH
EXPERTS = 4
EXTRA = 128
TILE = 256


def remote(src, dst, send_sem, recv_sem, target):
    return pltpu.make_async_remote_copy(
        src_ref=src,
        dst_ref=dst,
        send_sem=send_sem,
        recv_sem=recv_sem,
        device_id={"ep": target},
        device_id_type=MESH,
    )


def kernel(
    n, columns, chunks,
    tok, routes, weights, live, wg_hbm, wu_hbm, wd_hbm, out,
    xb, wg, wu, wd, hid, row_w, pf, pb, sb, got_r, got_l, put_r, put_l,
    w_sem, d_sem, ag_ss, ag_rs, sib_ss, sib_rs, rs_ss, rs_rs, sx_ss, sx_rs,
):
    rows, feat = tok.shape
    chips = n // 2
    half = chips // 2
    me = lax.axis_index("ep")
    core, chip = me % 2, me // 2
    depth = chips // columns
    if columns == 2:
        y, z = chip % 2, chip // 2
        ring = (1 - y) * z + y * (chips - 1 - z)
    else:
        ring = chip

    def device_at(pos):
        pos = (pos + chips) % chips
        if columns == 2:
            y = pos // depth
            z = (1 - y) * pos + y * (chips - 1 - pos)
            where = z * 2 + y
        else:
            where = pos
        return where * 2 + core

    right, left, sibling = device_at(ring + 1), device_at(ring - 1), chip * 2 + (1 - core)

    hid_tiles = wg.shape[0]
    out_tiles = wd.shape[0]

    def w_copy(j, which):
        src, dst = ((wg_hbm, wg), (wu_hbm, wu))[which]
        cols = pl.ds(pl.multiple_of(j * TILE, TILE), TILE)
        return pltpu.make_async_copy(src.at[:, cols], dst.at[j], w_sem.at[which, j])

    def d_copy(j):
        cols = pl.ds(pl.multiple_of(j * TILE, TILE), TILE)
        return pltpu.make_async_copy(wd_hbm.at[:, cols], wd.at[j], d_sem.at[j])

    for j in range(hid_tiles):
        w_copy(j, 0).start()
        w_copy(j, 1).start()
    for j in range(out_tiles):
        d_copy(j).start()

    barrier = pltpu.get_barrier_semaphore()
    for peer in (right, left, sibling):
        pl.semaphore_signal(barrier, inc=1, device_id={"ep": peer}, device_id_type=MESH)

    def block(pos, side):
        pos = (pos + chips) % chips
        return pl.ds(pl.multiple_of((side * chips + pos) * rows, rows), rows)

    mine = block(ring, core)
    xb[mine, pl.ds(0, feat)] = tok[...]
    is_live = lax.broadcasted_iota(jnp.int32, (rows, EXTRA), 0) < live[0]
    lane = lax.broadcasted_iota(jnp.int32, (rows, EXTRA), 1)
    which_expert = lane % EXPERTS
    combined = jnp.zeros((rows, EXTRA), jnp.float32)
    for k in range(2):
        combined += jnp.where(
            (routes[:, k : k + 1] == which_expert) & is_live, weights[:, k : k + 1], 0.0
        )
    high = combined.astype(jnp.bfloat16).astype(jnp.float32)
    middle = (combined - high).astype(jnp.bfloat16).astype(jnp.float32)
    low = combined - high - middle
    term = lane // EXPERTS
    packed = jnp.where(term == 0, high, jnp.where(term == 1, middle, jnp.where(term == 2, low, 0.0)))
    xb[mine, pl.ds(feat, EXTRA)] = packed.astype(jnp.bfloat16)

    pl.semaphore_wait(barrier, 3)

    width = feat + EXTRA
    split = (width // 2 + 127) // 128 * 128
    spans = (pl.ds(0, split), pl.ds(split, width - split))
    sent = []

    def ag_send(direction, step):
        pos = ring - (step - 1) if direction == 0 else ring + (step - 1)
        where = block(pos, core)
        view = xb.at[where] if step < half else xb.at[where, spans[direction]]
        copy = remote(
            view, view, ag_ss.at[direction, step - 1], ag_rs.at[direction, step - 1],
            right if direction == 0 else left,
        )
        copy.start()
        sent.append(copy)

    def ag_wait(direction, step):
        pos = ring - step if direction == 0 else ring + step
        where = block(pos, core)
        view = xb.at[where] if step < half else xb.at[where, spans[direction]]
        remote(
            view, view, ag_ss.at[direction, step - 1], ag_rs.at[direction, step - 1],
            right if direction == 0 else left,
        ).wait_recv()

    def sib_copy(offset, side):
        view = xb.at[block(ring + offset, side)]
        slot = (offset + chips) % chips
        return remote(view, view, sib_ss.at[slot], sib_rs.at[slot], sibling)

    def sib_send(offset):
        copy = sib_copy(offset, core)
        copy.start()
        sent.append(copy)

    ag_send(0, 1)
    ag_send(1, 1)
    sib_send(0)
    for step in range(1, half + 1):
        for direction in range(2):
            ag_wait(direction, step)
            if step < half:
                ag_send(direction, step + 1)
                sib_send(step if direction == 1 else -step)
    sib_send(half)
    for offset in range(chips):
        sib_copy(offset, 1 - core).wait_recv()

    expert = me // (n // EXPERTS)
    tail = xb[:, pl.ds(feat, EXTRA)].astype(jnp.float32)
    lanes = lax.broadcasted_iota(jnp.int32, tail.shape, 1)
    row_w[...] = jnp.sum(
        jnp.where(lanes % EXPERTS == expert, tail, 0.0), axis=1, keepdims=True
    )

    def hidden_tile(j, carry):
        w_copy(j, 0).wait()
        w_copy(j, 1).wait()
        x = xb[:, pl.ds(0, feat)]
        gate = jnp.dot(x, wg[j], preferred_element_type=jnp.float32)
        upward = jnp.dot(x, wu[j], preferred_element_type=jnp.float32)
        hid[:, pl.ds(pl.multiple_of(j * TILE, TILE), TILE)] = (
            gate / (1.0 + jnp.exp(-gate)) * upward
        ).astype(jnp.bfloat16)
        return carry

    lax.fori_loop(0, hid_tiles, hidden_tile, 0)

    per_chunk = out_tiles // chunks
    chunk = per_chunk * TILE
    cut = (chunk // 2 + 127) // 128 * 128
    parts = (pl.ds(0, cut), pl.ds(cut, chunk - cut))
    side_rows = chips * rows

    def side_span(side):
        return pl.ds(pl.multiple_of(side * side_rows, side_rows), side_rows)

    def sx_copy(k):
        return remote(pb.at[k, side_span(1 - core)], sb.at[k], sx_ss.at[k], sx_rs.at[k], sibling)

    def local_sum(k, pos, cols):
        pos = (pos + chips) % chips
        return pf[k, block(pos, core), cols] + sb[
            k, pl.ds(pl.multiple_of(pos * rows, rows), rows), cols
        ].astype(jnp.float32)

    whole = pl.ds(0, chunk)

    def rs_copy(direction, k, step):
        src, dst = ((put_r, got_r), (put_l, got_l))[direction]
        src, dst = src.at[k, step - 1], dst.at[k, step - 1]
        if step == 1:
            src, dst = src.at[:, parts[direction]], dst.at[:, parts[direction]]
        return remote(
            src, dst, rs_ss.at[direction, k, step - 1], rs_rs.at[direction, k, step - 1],
            right if direction == 0 else left,
        )

    def rs_step(k, step):
        for direction in range(2):
            put, got = ((put_r, got_r), (put_l, got_l))[direction]
            away = half - step + 1
            pos = ring + away if direction == 0 else ring - away
            if step == 1:
                put[k, 0, :, parts[direction]] = local_sum(k, pos, parts[direction]).astype(jnp.bfloat16)
            else:
                rs_copy(direction, k, step - 1).wait_recv()
                if step == 2:
                    here, other = parts[direction], parts[1 - direction]
                    put[k, 1, :, here] = (
                        local_sum(k, pos, here) + got[k, 0, :, here].astype(jnp.float32)
                    ).astype(jnp.bfloat16)
                    put[k, 1, :, other] = local_sum(k, pos, other).astype(jnp.bfloat16)
                else:
                    put[k, step - 1] = (
                        local_sum(k, pos, whole) + got[k, step - 2].astype(jnp.float32)
                    ).astype(jnp.bfloat16)
            copy = rs_copy(direction, k, step)
            copy.start()
            sent.append(copy)

    def open_ring(k):
        sx_copy(k).wait_recv()
        rs_step(k, 1)

    for k in range(chunks):

        def out_tile(t, carry, k=k):
            j = k * per_chunk + t
            d_copy(j).wait()
            cols = pl.ds(pl.multiple_of(t * TILE, TILE), TILE)
            value = jnp.dot(hid[...], wd[j], preferred_element_type=jnp.float32) * row_w[...]
            pf[k, :, cols] = value
            pb[k, :, cols] = value.astype(jnp.bfloat16)
            return carry

        lax.fori_loop(0, per_chunk, out_tile, 0)
        copy = sx_copy(k)
        copy.start()
        sent.append(copy)
        if k > 0:
            open_ring(k - 1)
    open_ring(chunks - 1)
    for step in range(2, half + 1):
        for k in range(chunks):
            rs_step(k, step)
    for k in range(chunks):
        rs_copy(0, k, half).wait_recv()
        rs_copy(1, k, half).wait_recv()
        total = (
            local_sum(k, ring, whole)
            + got_r[k, half - 1].astype(jnp.float32)
            + got_l[k, half - 1].astype(jnp.float32)
        )
        out[:, pl.ds(k * chunk, chunk)] = total.astype(jnp.bfloat16)
    for copy in sent:
        copy.wait_send()


def local(n, tokens, routes, route_weights, live_counts, w_gate, w_up, w_down):
    rows, feat = tokens.shape
    share = w_gate.shape[1]
    chips = n // 2
    half = chips // 2
    columns = 2 if chips <= 8 else 1
    chunks = 3
    chunk = feat // chunks
    all_rows = n * rows
    vmem = pl.BlockSpec(memory_space=pltpu.VMEM)
    hbm = pl.BlockSpec(memory_space=pl.ANY)
    bf16, f32 = jnp.bfloat16, jnp.float32
    ring_buffer = pltpu.VMEM((chunks, half, rows, chunk), bf16)
    dma = pltpu.SemaphoreType.DMA
    return pl.pallas_call(
        functools.partial(kernel, n, columns, chunks),
        out_shape=jax.ShapeDtypeStruct((rows, feat), bf16),
        in_specs=[vmem, vmem, vmem, pl.BlockSpec(memory_space=pltpu.SMEM), hbm, hbm, hbm],
        out_specs=vmem,
        scratch_shapes=[
            pltpu.VMEM((all_rows, feat + EXTRA), bf16),
            pltpu.VMEM((share // TILE, feat, TILE), bf16),
            pltpu.VMEM((share // TILE, feat, TILE), bf16),
            pltpu.VMEM((feat // TILE, share, TILE), bf16),
            pltpu.VMEM((all_rows, share), bf16),
            pltpu.VMEM((all_rows, 1), f32),
            pltpu.VMEM((chunks, all_rows, chunk), f32),
            pltpu.VMEM((chunks, all_rows, chunk), bf16),
            pltpu.VMEM((chunks, chips * rows, chunk), bf16),
            ring_buffer, ring_buffer, ring_buffer, ring_buffer,
            dma((2, share // TILE)),
            dma((feat // TILE,)),
            dma((2, half)), dma((2, half)),
            dma((chips,)), dma((chips,)),
            dma((2, chunks, half)), dma((2, chunks, half)),
            dma((chunks,)), dma((chunks,)),
        ],
        compiler_params=pltpu.CompilerParams(
            collective_id=0, has_side_effects=True, vmem_limit_bytes=60 * 2**20
        ),
    )(tokens, routes, route_weights, live_counts, w_gate, w_up, w_down)


def solution(mesh):
    in_specs = (
        P(("groups", "ep"), None),
        P(("groups", "ep"), None),
        P(("groups", "ep"), None),
        P(("groups", "ep")),
        P(None, "ep"),
        P(None, "ep"),
        P("ep", None),
    )
    return jax.shard_map(
        functools.partial(local, mesh.shape["ep"]),
        mesh=mesh, in_specs=in_specs, out_specs=P(("groups", "ep"), None), check_vma=False,
    )
```

```python
import functools

import jax
import jax.numpy as jnp
from jax import lax
from jax.experimental import pallas as pl
from jax.experimental.pallas import tpu as pltpu
from jax.sharding import PartitionSpec as P

MESH = pl.DeviceIdType.MESH
EXPERTS = 4
EXTRA = 128
TILE = 256


def remote(src, dst, send_sem, recv_sem, target):
    return pltpu.make_async_remote_copy(
        src_ref=src,
        dst_ref=dst,
        send_sem=send_sem,
        recv_sem=recv_sem,
        device_id={"ep": target},
        device_id_type=MESH,
    )


def kernel(
    n, columns, chunks,
    tok, routes, weights, live, wg_hbm, wu_hbm, wd_hbm, out,
    xb, wg, wu, wd, hid, row_w, pf, pb, sb, got_r, got_l, put_r, put_l,
    w_sem, d_sem, ag_ss, ag_rs, sib_ss, sib_rs, rs_ss, rs_rs, sx_ss, sx_rs,
):
    rows, feat = tok.shape
    chips = n // 2
    half = chips // 2
    me = lax.axis_index("ep")
    core, chip = me % 2, me // 2
    depth = chips // columns
    if columns == 2:
        y, z = chip % 2, chip // 2
        ring = (1 - y) * z + y * (chips - 1 - z)
    else:
        ring = chip

    def device_at(pos):
        pos = (pos + chips) % chips
        if columns == 2:
            y = pos // depth
            z = (1 - y) * pos + y * (chips - 1 - pos)
            where = z * 2 + y
        else:
            where = pos
        return where * 2 + core

    right, left, sibling = device_at(ring + 1), device_at(ring - 1), chip * 2 + (1 - core)

    hid_tiles = wg.shape[0]
    out_tiles = wd.shape[0]

    def w_copy(j, which):
        src, dst = ((wg_hbm, wg), (wu_hbm, wu))[which]
        cols = pl.ds(pl.multiple_of(j * TILE, TILE), TILE)
        return pltpu.make_async_copy(src.at[:, cols], dst.at[j], w_sem.at[which, j])

    def d_copy(j):
        cols = pl.ds(pl.multiple_of(j * TILE, TILE), TILE)
        return pltpu.make_async_copy(wd_hbm.at[:, cols], wd.at[j], d_sem.at[j])

    for j in range(hid_tiles):
        w_copy(j, 0).start()
        w_copy(j, 1).start()
    for j in range(out_tiles):
        d_copy(j).start()

    barrier = pltpu.get_barrier_semaphore()
    for peer in (right, left, sibling):
        pl.semaphore_signal(barrier, inc=1, device_id={"ep": peer}, device_id_type=MESH)

    near = half // 2
    groups = (
        [d for d in range(-near, near + 1)],
        [d for d in range(near + 1, half)] + [half] + [-d for d in range(near + 1, half)],
    )
    counts = [len(g) * rows for g in groups]
    starts = [0, 2 * counts[0]]

    def home(rel):
        rel = half if rel == -half else rel
        g = 0 if rel in groups[0] else 1
        return g, groups[g].index(rel)

    def slot(rel, side):
        g, i = home(rel)
        return pl.ds(starts[g] + side * counts[g] + i * rows, rows)

    def side_row(rel):
        g, i = home(rel)
        return pl.ds((counts[0] if g else 0) + i * rows, rows)

    xb[slot(0, 0), pl.ds(0, feat)] = tok[...]
    diagonal = lax.broadcasted_iota(jnp.int32, (rows, rows), 0) == lax.broadcasted_iota(
        jnp.int32, (rows, rows), 1
    )

    def column(ref, k):
        spread = jnp.broadcast_to(ref[k : k + 1, :].astype(jnp.float32), (rows, rows))
        return jnp.sum(jnp.where(diagonal, spread, 0.0), axis=1, keepdims=True)

    is_live = lax.broadcasted_iota(jnp.int32, (rows, EXTRA), 0) < live[0]
    lane = lax.broadcasted_iota(jnp.int32, (rows, EXTRA), 1)
    which_expert = lane % EXPERTS
    combined = jnp.zeros((rows, EXTRA), jnp.float32)
    for k in range(2):
        combined += jnp.where(
            (column(routes, k).astype(jnp.int32) == which_expert) & is_live, column(weights, k), 0.0
        )
    high = combined.astype(jnp.bfloat16).astype(jnp.float32)
    middle = (combined - high).astype(jnp.bfloat16).astype(jnp.float32)
    low = combined - high - middle
    term = lane // EXPERTS
    packed = jnp.where(term == 0, high, jnp.where(term == 1, middle, jnp.where(term == 2, low, 0.0)))
    xb[slot(0, 0), pl.ds(feat, EXTRA)] = packed.astype(jnp.bfloat16)

    pl.semaphore_wait(barrier, 3)

    width = feat + EXTRA
    split = (width // 2 + 127) // 128 * 128
    spans = (pl.ds(0, split), pl.ds(split, width - split))
    sent = []

    def go(copy):
        copy.start()
        sent.append(copy)

    def ag_copy(direction, step):
        sign = -1 if direction == 0 else 1
        src, dst = slot(sign * (step - 1), 0), slot(sign * step, 0)
        if step == half:
            src, dst = (src, spans[direction]), (dst, spans[direction])
        return remote(
            xb.at[src], xb.at[dst], ag_ss.at[direction, step - 1], ag_rs.at[direction, step - 1],
            right if direction == 0 else left,
        )

    def sib_copy(rel):
        i = rel % chips
        return remote(xb.at[slot(rel, 0)], xb.at[slot(rel, 1)], sib_ss.at[i], sib_rs.at[i], sibling)

    def ag_step(step):
        for direction in range(2):
            ag_copy(direction, step).wait_recv()
            if step < half:
                go(ag_copy(direction, step + 1))
                go(sib_copy(-step if direction == 0 else step))
        if step == half:
            go(sib_copy(half))

    expert = me // (n // EXPERTS)
    spots = [pl.ds(starts[g], 2 * counts[g]) for g in range(2)]

    def weigh(g):
        for rel in groups[g]:
            sib_copy(rel).wait_recv()
        tail = xb[spots[g], pl.ds(feat, EXTRA)].astype(jnp.float32)
        lanes = lax.broadcasted_iota(jnp.int32, tail.shape, 1)
        row_w[spots[g], :] = jnp.sum(
            jnp.where(lanes % EXPERTS == expert, tail, 0.0), axis=1, keepdims=True
        )

    def hidden_tiles(g, first, last):
        def tile(j, carry):
            if g == 0:
                w_copy(j, 0).wait()
                w_copy(j, 1).wait()
            x = xb[spots[g], pl.ds(0, feat)]
            gate = jnp.dot(x, wg[j], preferred_element_type=jnp.float32)
            upward = jnp.dot(x, wu[j], preferred_element_type=jnp.float32)
            hid[spots[g], pl.ds(pl.multiple_of(j * TILE, TILE), TILE)] = (
                gate / (1.0 + jnp.exp(-gate)) * upward
            ).astype(jnp.bfloat16)
            return carry

        if last > first:
            lax.fori_loop(first, last, tile, 0)

    go(ag_copy(0, 1))
    go(ag_copy(1, 1))
    go(sib_copy(0))
    for step in range(1, near + 1):
        ag_step(step)
    weigh(0)
    late = half - near
    for i in range(late):
        hidden_tiles(0, i * hid_tiles // late, (i + 1) * hid_tiles // late)
        ag_step(near + 1 + i)
    weigh(1)
    hidden_tiles(1, 0, hid_tiles)

    per_chunk = out_tiles // chunks
    chunk = per_chunk * TILE
    cut = (chunk // 2 + 127) // 128 * 128
    parts = (pl.ds(0, cut), pl.ds(cut, chunk - cut))
    whole = pl.ds(0, chunk)
    side_spots = (pl.ds(0, counts[0]), pl.ds(counts[0], counts[1]))

    def sx_copy(k, g):
        return remote(
            pb.at[k, side_spots[g]], sb.at[k, side_spots[g]], sx_ss.at[k, g], sx_rs.at[k, g], sibling
        )

    def out_tiles_of(k, g):
        def tile(t, carry):
            j = k * per_chunk + t
            if g == 1:
                d_copy(j).wait()
            cols = pl.ds(pl.multiple_of(t * TILE, TILE), TILE)
            value = jnp.dot(
                hid[spots[g], :], wd[j], preferred_element_type=jnp.float32
            ) * row_w[spots[g], :]
            pf[k, side_spots[g], cols] = value[: counts[g]]
            pb[k, side_spots[g], cols] = value[counts[g] :].astype(jnp.bfloat16)
            return carry

        lax.fori_loop(0, per_chunk, tile, 0)
        go(sx_copy(k, g))

    def local_sum(k, rel, cols):
        return pf[k, side_row(rel), cols] + sb[k, side_row(rel), cols].astype(jnp.float32)

    def rs_copy(direction, k, step):
        src, dst = ((put_r, got_r), (put_l, got_l))[direction]
        src, dst = src.at[k, step - 1], dst.at[k, step - 1]
        if step == 1:
            src, dst = src.at[:, parts[direction]], dst.at[:, parts[direction]]
        return remote(
            src, dst, rs_ss.at[direction, k, step - 1], rs_rs.at[direction, k, step - 1],
            right if direction == 0 else left,
        )

    def rs_step(k, step):
        for direction in range(2):
            put, got = ((put_r, got_r), (put_l, got_l))[direction]
            away = half - step + 1
            rel = away if direction == 0 else -away
            if step == 1:
                put[k, 0, :, parts[direction]] = local_sum(k, rel, parts[direction]).astype(jnp.bfloat16)
            else:
                rs_copy(direction, k, step - 1).wait_recv()
                if step == 2:
                    here, other = parts[direction], parts[1 - direction]
                    put[k, 1, :, here] = (
                        local_sum(k, rel, here) + got[k, 0, :, here].astype(jnp.float32)
                    ).astype(jnp.bfloat16)
                    put[k, 1, :, other] = local_sum(k, rel, other).astype(jnp.bfloat16)
                else:
                    put[k, step - 1] = (
                        local_sum(k, rel, whole) + got[k, step - 2].astype(jnp.float32)
                    ).astype(jnp.bfloat16)
            go(rs_copy(direction, k, step))

    def open_ring(k):
        sx_copy(k, 1).wait_recv()
        rs_step(k, 1)

    for k in range(chunks):
        out_tiles_of(k, 1)
        if k > 0:
            open_ring(k - 1)
    out_tiles_of(0, 0)
    open_ring(chunks - 1)
    for k in range(1, chunks):
        out_tiles_of(k, 0)
        rs_step(k - 1, 2)
    rs_step(chunks - 1, 2)
    for k in range(chunks):
        sx_copy(k, 0).wait_recv()
    for step in range(3, half + 1):
        for k in range(chunks):
            rs_step(k, step)
    for k in range(chunks):
        rs_copy(0, k, half).wait_recv()
        rs_copy(1, k, half).wait_recv()
        total = (
            local_sum(k, 0, whole)
            + got_r[k, half - 1].astype(jnp.float32)
            + got_l[k, half - 1].astype(jnp.float32)
        )
        out[:, pl.ds(k * chunk, chunk)] = total.astype(jnp.bfloat16)
    for copy in sent:
        copy.wait_send()


def local(n, tokens, routes, route_weights, live_counts, w_gate, w_up, w_down):
    rows, feat = tokens.shape
    share = w_gate.shape[1]
    chips = n // 2
    half = chips // 2
    columns = 2 if chips <= 8 else 1
    chunks = 3
    chunk = feat // chunks
    all_rows = n * rows
    vmem = pl.BlockSpec(memory_space=pltpu.VMEM)
    hbm = pl.BlockSpec(memory_space=pl.ANY)
    bf16, f32 = jnp.bfloat16, jnp.float32
    ring_buffer = pltpu.VMEM((chunks, half, rows, chunk), bf16)
    dma = pltpu.SemaphoreType.DMA
    return pl.pallas_call(
        functools.partial(kernel, n, columns, chunks),
        out_shape=jax.ShapeDtypeStruct((rows, feat), bf16),
        in_specs=[vmem, vmem, vmem, pl.BlockSpec(memory_space=pltpu.SMEM), hbm, hbm, hbm],
        out_specs=vmem,
        scratch_shapes=[
            pltpu.VMEM((all_rows, feat + EXTRA), bf16),
            pltpu.VMEM((share // TILE, feat, TILE), bf16),
            pltpu.VMEM((share // TILE, feat, TILE), bf16),
            pltpu.VMEM((feat // TILE, share, TILE), bf16),
            pltpu.VMEM((all_rows, share), bf16),
            pltpu.VMEM((all_rows, 1), f32),
            pltpu.VMEM((chunks, chips * rows, chunk), f32),
            pltpu.VMEM((chunks, chips * rows, chunk), bf16),
            pltpu.VMEM((chunks, chips * rows, chunk), bf16),
            ring_buffer, ring_buffer, ring_buffer, ring_buffer,
            dma((2, share // TILE)),
            dma((feat // TILE,)),
            dma((2, half)), dma((2, half)),
            dma((chips,)), dma((chips,)),
            dma((2, chunks, half)), dma((2, chunks, half)),
            dma((chunks, 2)), dma((chunks, 2)),
        ],
        compiler_params=pltpu.CompilerParams(
            collective_id=0, has_side_effects=True, vmem_limit_bytes=60 * 2**20
        ),
    )(tokens, routes.T, route_weights.T, live_counts, w_gate, w_up, w_down)


def solution(mesh):
    in_specs = (
        P(("groups", "ep"), None),
        P(("groups", "ep"), None),
        P(("groups", "ep"), None),
        P(("groups", "ep")),
        P(None, "ep"),
        P(None, "ep"),
        P("ep", None),
    )
    return jax.shard_map(
        functools.partial(local, mesh.shape["ep"]),
        mesh=mesh, in_specs=in_specs, out_specs=P(("groups", "ep"), None), check_vma=False,
    )
```

```python
import functools

import jax
import jax.numpy as jnp
from jax import lax
from jax.experimental import pallas as pl
from jax.experimental.pallas import tpu as pltpu
from jax.sharding import PartitionSpec as P

MESH = pl.DeviceIdType.MESH
EXPERTS = 4
EXTRA = 128
TILE = 256


def remote(src, dst, send_sem, recv_sem, target):
    return pltpu.make_async_remote_copy(
        src_ref=src,
        dst_ref=dst,
        send_sem=send_sem,
        recv_sem=recv_sem,
        device_id={"ep": target},
        device_id_type=MESH,
    )


def kernel(
    n, columns, chunks,
    tok, routes, weights, live, wg_hbm, wu_hbm, wd_hbm, out,
    xb, wg, wu, wd, hid, row_w, pf, pb, sb, got_r, got_l, put_r, put_l,
    w_sem, d_sem, ag_ss, ag_rs, sib_ss, sib_rs, rs_ss, rs_rs, sx_ss, sx_rs,
):
    rows, feat = tok.shape
    chips = n // 2
    half = chips // 2
    me = lax.axis_index("ep")
    core, chip = me % 2, me // 2
    depth = chips // columns
    if columns == 2:
        y, z = chip % 2, chip // 2
        ring = (1 - y) * z + y * (chips - 1 - z)
    else:
        ring = chip

    def device_at(pos):
        pos = (pos + chips) % chips
        if columns == 2:
            y = pos // depth
            z = (1 - y) * pos + y * (chips - 1 - pos)
            where = z * 2 + y
        else:
            where = pos
        return where * 2 + core

    sibling = chip * 2 + (1 - core)
    ahead = (
        (device_at(ring + 1), device_at(ring + 2)),
        (device_at(ring - 1), device_at(ring - 2)),
    )

    hid_tiles = wg.shape[0]
    out_tiles = wd.shape[0]

    def w_copy(j, which):
        src, dst = ((wg_hbm, wg), (wu_hbm, wu))[which]
        cols = pl.ds(pl.multiple_of(j * TILE, TILE), TILE)
        return pltpu.make_async_copy(src.at[:, cols], dst.at[j], w_sem.at[which, j])

    def d_copy(j):
        cols = pl.ds(pl.multiple_of(j * TILE, TILE), TILE)
        return pltpu.make_async_copy(wd_hbm.at[:, cols], wd.at[j], d_sem.at[j])

    for j in range(hid_tiles):
        w_copy(j, 0).start()
        w_copy(j, 1).start()
    for j in range(out_tiles):
        d_copy(j).start()

    barrier = pltpu.get_barrier_semaphore()
    for peer in ahead[0] + ahead[1] + (sibling,):
        pl.semaphore_signal(barrier, inc=1, device_id={"ep": peer}, device_id_type=MESH)

    near = half // 2
    groups = (
        [d for d in range(-near, near + 1)],
        [d for d in range(near + 1, half)] + [half] + [-d for d in range(near + 1, half)],
    )
    counts = [len(g) * rows for g in groups]
    starts = [0, 2 * counts[0]]

    def home(rel):
        rel = half if rel == -half else rel
        g = 0 if rel in groups[0] else 1
        return g, groups[g].index(rel)

    def slot(rel, side):
        g, i = home(rel)
        return pl.ds(starts[g] + side * counts[g] + i * rows, rows)

    def side_row(rel):
        g, i = home(rel)
        return pl.ds((counts[0] if g else 0) + i * rows, rows)

    xb[slot(0, 0), pl.ds(0, feat)] = tok[...]
    diagonal = lax.broadcasted_iota(jnp.int32, (rows, rows), 0) == lax.broadcasted_iota(
        jnp.int32, (rows, rows), 1
    )

    def column(ref, k):
        spread = jnp.broadcast_to(ref[k : k + 1, :].astype(jnp.float32), (rows, rows))
        return jnp.sum(jnp.where(diagonal, spread, 0.0), axis=1, keepdims=True)

    is_live = lax.broadcasted_iota(jnp.int32, (rows, EXTRA), 0) < live[0]
    lane = lax.broadcasted_iota(jnp.int32, (rows, EXTRA), 1)
    which_expert = lane % EXPERTS
    combined = jnp.zeros((rows, EXTRA), jnp.float32)
    for k in range(2):
        combined += jnp.where(
            (column(routes, k).astype(jnp.int32) == which_expert) & is_live, column(weights, k), 0.0
        )
    high = combined.astype(jnp.bfloat16).astype(jnp.float32)
    middle = (combined - high).astype(jnp.bfloat16).astype(jnp.float32)
    low = combined - high - middle
    term = lane // EXPERTS
    packed = jnp.where(term == 0, high, jnp.where(term == 1, middle, jnp.where(term == 2, low, 0.0)))
    xb[slot(0, 0), pl.ds(feat, EXTRA)] = packed.astype(jnp.bfloat16)

    pl.semaphore_wait(barrier, 5)

    width = feat + EXTRA
    split = (width // 2 + 127) // 128 * 128
    spans = (pl.ds(0, split), pl.ds(split, width - split))
    sent = []

    def go(copy):
        copy.start()
        sent.append(copy)

    def ag_copy(direction, step):
        sign = -1 if direction == 0 else 1
        src, dst = slot(sign * (step - 1), 0), slot(sign * step, 0)
        if step == half:
            src, dst = (src, spans[direction]), (dst, spans[direction])
        return remote(
            xb.at[src], xb.at[dst], ag_ss.at[direction, step - 1], ag_rs.at[direction, step - 1],
            ahead[direction][0],
        )

    def sib_copy(rel):
        i = rel % chips
        return remote(xb.at[slot(rel, 0)], xb.at[slot(rel, 1)], sib_ss.at[i], sib_rs.at[i], sibling)

    def ag_step(step):
        for direction in range(2):
            ag_copy(direction, step).wait_recv()
            if step < half:
                go(ag_copy(direction, step + 1))
                go(sib_copy(-step if direction == 0 else step))
        if step == half:
            go(sib_copy(half))

    expert = me // (n // EXPERTS)
    spots = [pl.ds(starts[g], 2 * counts[g]) for g in range(2)]

    def weigh(g):
        for rel in groups[g]:
            sib_copy(rel).wait_recv()
        tail = xb[spots[g], pl.ds(feat, EXTRA)].astype(jnp.float32)
        lanes = lax.broadcasted_iota(jnp.int32, tail.shape, 1)
        row_w[spots[g], :] = jnp.sum(
            jnp.where(lanes % EXPERTS == expert, tail, 0.0), axis=1, keepdims=True
        )

    def hidden_tiles(g, first, last):
        def tile(j, carry):
            if g == 0:
                w_copy(j, 0).wait()
                w_copy(j, 1).wait()
            x = xb[spots[g], pl.ds(0, feat)]
            gate = jnp.dot(x, wg[j], preferred_element_type=jnp.float32)
            upward = jnp.dot(x, wu[j], preferred_element_type=jnp.float32)
            hid[spots[g], pl.ds(pl.multiple_of(j * TILE, TILE), TILE)] = (
                gate / (1.0 + jnp.exp(-gate)) * upward
            ).astype(jnp.bfloat16)
            return carry

        if last > first:
            lax.fori_loop(first, last, tile, 0)

    go(ag_copy(0, 1))
    go(ag_copy(1, 1))
    go(sib_copy(0))
    for step in range(1, near + 1):
        ag_step(step)
    weigh(0)
    late = half - near
    for i in range(late):
        hidden_tiles(0, i * hid_tiles // late, (i + 1) * hid_tiles // late)
        ag_step(near + 1 + i)
    weigh(1)
    hidden_tiles(1, 0, hid_tiles)

    per_chunk = out_tiles // chunks
    chunk = per_chunk * TILE
    cut = (chunk // 2 + 127) // 128 * 128
    parts = (pl.ds(0, cut), pl.ds(cut, chunk - cut))
    whole = pl.ds(0, chunk)
    side_spots = (pl.ds(0, counts[0]), pl.ds(counts[0], counts[1]))

    def sx_copy(k, g):
        return remote(
            pb.at[k, side_spots[g]], sb.at[k, side_spots[g]], sx_ss.at[k, g], sx_rs.at[k, g], sibling
        )

    def out_tiles_of(k, g):
        def tile(t, carry):
            j = k * per_chunk + t
            if g == 1:
                d_copy(j).wait()
            cols = pl.ds(pl.multiple_of(t * TILE, TILE), TILE)
            value = jnp.dot(
                hid[spots[g], :], wd[j], preferred_element_type=jnp.float32
            ) * row_w[spots[g], :]
            pf[k, side_spots[g], cols] = value[: counts[g]]
            pb[k, side_spots[g], cols] = value[counts[g] :].astype(jnp.bfloat16)
            return carry

        lax.fori_loop(0, per_chunk, tile, 0)
        go(sx_copy(k, g))

    def local_sum(k, rel, cols):
        return pf[k, side_row(rel), cols] + sb[k, side_row(rel), cols].astype(jnp.float32)

    def rs_copy(direction, k, away):
        src, dst = ((put_r, got_r), (put_l, got_l))[direction]
        src, dst = src.at[k, away - 1], dst.at[k, away - 1]
        if away == half:
            src, dst = src.at[:, parts[direction]], dst.at[:, parts[direction]]
        return remote(
            src, dst, rs_ss.at[direction, k, away - 1], rs_rs.at[direction, k, away - 1],
            ahead[direction][1 - away % 2],
        )

    def rs_send(k, away):
        for direction in range(2):
            put, got = ((put_r, got_r), (put_l, got_l))[direction]
            rel = away if direction == 0 else -away
            here, other = parts[direction], parts[1 - direction]
            if away == half:
                put[k, away - 1, :, here] = local_sum(k, rel, here).astype(jnp.bfloat16)
            elif away % 2 == 1:
                put[k, away - 1] = local_sum(k, rel, whole).astype(jnp.bfloat16)
            else:
                rs_copy(direction, k, away + 1).wait_recv()
                rs_copy(direction, k, away + 2).wait_recv()
                for cols in (here, other):
                    value = local_sum(k, rel, cols) + got[k, away, :, cols].astype(jnp.float32)
                    if away + 2 < half or cols is here:
                        value += got[k, away + 1, :, cols].astype(jnp.float32)
                    put[k, away - 1, :, cols] = value.astype(jnp.bfloat16)
            go(rs_copy(direction, k, away))

    def rs_group(k, g):
        sx_copy(k, g).wait_recv()
        members = [d for d in groups[g] if d > 0]
        if half in members:
            rs_send(k, half)
        for away in sorted(d for d in members if d % 2 == 1):
            rs_send(k, away)

    def rs_relay(k, g):
        for away in sorted((d for d in groups[g] if 0 < d < half and d % 2 == 0), reverse=True):
            rs_send(k, away)

    for k in range(chunks):
        out_tiles_of(k, 1)
        if k > 0:
            rs_group(k - 1, 1)
    out_tiles_of(0, 0)
    rs_group(chunks - 1, 1)
    for k in range(1, chunks):
        out_tiles_of(k, 0)
        rs_group(k - 1, 0)
        rs_relay(k - 1, 1)
        rs_relay(k - 1, 0)
    rs_group(chunks - 1, 0)
    rs_relay(chunks - 1, 1)
    rs_relay(chunks - 1, 0)
    for k in range(chunks):
        total = local_sum(k, 0, whole)
        for direction in range(2):
            for away in (1, 2):
                rs_copy(direction, k, away).wait_recv()
                total += (got_r, got_l)[direction][k, away - 1].astype(jnp.float32)
        out[:, pl.ds(k * chunk, chunk)] = total.astype(jnp.bfloat16)
    for copy in sent:
        copy.wait_send()


def local(n, tokens, routes, route_weights, live_counts, w_gate, w_up, w_down):
    rows, feat = tokens.shape
    share = w_gate.shape[1]
    chips = n // 2
    half = chips // 2
    columns = 2 if chips <= 8 else 1
    chunks = 3
    chunk = feat // chunks
    all_rows = n * rows
    vmem = pl.BlockSpec(memory_space=pltpu.VMEM)
    hbm = pl.BlockSpec(memory_space=pl.ANY)
    bf16, f32 = jnp.bfloat16, jnp.float32
    ring_buffer = pltpu.VMEM((chunks, half, rows, chunk), bf16)
    dma = pltpu.SemaphoreType.DMA
    return pl.pallas_call(
        functools.partial(kernel, n, columns, chunks),
        out_shape=jax.ShapeDtypeStruct((rows, feat), bf16),
        in_specs=[vmem, vmem, vmem, pl.BlockSpec(memory_space=pltpu.SMEM), hbm, hbm, hbm],
        out_specs=vmem,
        scratch_shapes=[
            pltpu.VMEM((all_rows, feat + EXTRA), bf16),
            pltpu.VMEM((share // TILE, feat, TILE), bf16),
            pltpu.VMEM((share // TILE, feat, TILE), bf16),
            pltpu.VMEM((feat // TILE, share, TILE), bf16),
            pltpu.VMEM((all_rows, share), bf16),
            pltpu.VMEM((all_rows, 1), f32),
            pltpu.VMEM((chunks, chips * rows, chunk), f32),
            pltpu.VMEM((chunks, chips * rows, chunk), bf16),
            pltpu.VMEM((chunks, chips * rows, chunk), bf16),
            ring_buffer, ring_buffer, ring_buffer, ring_buffer,
            dma((2, share // TILE)),
            dma((feat // TILE,)),
            dma((2, half)), dma((2, half)),
            dma((chips,)), dma((chips,)),
            dma((2, chunks, half)), dma((2, chunks, half)),
            dma((chunks, 2)), dma((chunks, 2)),
        ],
        compiler_params=pltpu.CompilerParams(
            collective_id=0, has_side_effects=True, vmem_limit_bytes=60 * 2**20
        ),
    )(tokens, routes.T, route_weights.T, live_counts, w_gate, w_up, w_down)


def solution(mesh):
    in_specs = (
        P(("groups", "ep"), None),
        P(("groups", "ep"), None),
        P(("groups", "ep"), None),
        P(("groups", "ep")),
        P(None, "ep"),
        P(None, "ep"),
        P("ep", None),
    )
    return jax.shard_map(
        functools.partial(local, mesh.shape["ep"]),
        mesh=mesh, in_specs=in_specs, out_specs=P(("groups", "ep"), None), check_vma=False,
    )
```
